32 devices in a mesh: dp: 8 (over z, x), mp: 4 (over y, core).
Axes of the slice: x: 2, y: 2, z: 4, core: 2. Of those that a mesh axis runs over, the one named last changes fastest.
Arguments:
- tokens: bfloat16 [8192, 2048], P(('dp', 'mp')), may hold values from -6 to 6
- cotangent: bfloat16 [8192, 2048], P(('dp', 'mp')), as said below
- gains_master: float32 [2, 2048], replicated, may hold values from 0.5 to 1.5
- scoring_master: float32 [2, 2048, 2048], P(None, 'dp', 'mp'), as said below
- mixing_master: float32 [2, 2048, 4096], P(None, 'dp', 'mp'), as said below
- output_master: float32 [4096, 2048], P(('mp', 'dp')), as said below
- expand_master: float32 [2048, 4096], P('dp', 'mp'), as said below
- shrink_master: float32 [4096, 2048], P(('mp', 'dp')), as said below
- gains_first: float32 [2, 2048], replicated, may hold values from -64 to 64
- gains_second: float32 [2, 2048], replicated, may hold values from 4.096 to 32.768
- scoring_first: float32 [2, 2048, 2048], P(None, 'dp', 'mp'), may hold values from -64 to 64
- scoring_second: float32 [2, 2048, 2048], P(None, 'dp', 'mp'), as said below
- mixing_first: float32 [2, 2048, 4096], P(None, 'dp', 'mp'), may hold values from -28 to 28
- mixing_second: float32 [2, 2048, 4096], P(None, 'dp', 'mp'), as said below
- output_first: float32 [4096, 2048], P(('mp', 'dp')), may hold values from -40 to 40
- output_second: float32 [4096, 2048], P(('mp', 'dp')), as said below
- expand_first: float32 [2048, 4096], P('dp', 'mp'), may hold values from -20 to 20
- expand_second: float32 [2048, 4096], P('dp', 'mp'), as said below
- shrink_first: float32 [4096, 2048], P(('mp', 'dp')), may hold values from -32 to 32
- shrink_second: float32 [4096, 2048], P(('mp', 'dp')), as said below
Outputs:
- layer_output: bfloat16 [8192, 2048], P(('dp', 'mp'))
- input_grad: float32 [8192, 2048], P(('dp', 'mp'))
- gains_grad: float32 [2, 2048], replicated
- scoring_grad: float32 [2, 2048, 2048], P(None, 'dp', 'mp')
- mixing_grad: float32 [2, 2048, 4096], P(None, 'dp', 'mp')
- output_grad: float32 [4096, 2048], P(('mp', 'dp'))
- expand_grad: float32 [2048, 4096], P('dp', 'mp')
- shrink_grad: float32 [4096, 2048], P(('mp', 'dp'))
- gains_moment: float32 [2, 2048], replicated
- scoring_moment: float32 [2, 2048, 2048], P(None, 'dp', 'mp')
- mixing_moment: float32 [2, 2048, 4096], P(None, 'dp', 'mp')
- output_moment: float32 [4096, 2048], P(('mp', 'dp'))
- expand_moment: float32 [2048, 4096], P('dp', 'mp')
- shrink_moment: float32 [4096, 2048], P(('mp', 'dp'))
- gains_square: float32 [2, 2048], replicated
- scoring_square: float32 [2, 2048, 2048], P(None, 'dp', 'mp')
- mixing_square: float32 [2, 2048, 4096], P(None, 'dp', 'mp')
- output_square: float32 [4096, 2048], P(('mp', 'dp'))
- expand_square: float32 [2048, 4096], P('dp', 'mp')
- shrink_square: float32 [4096, 2048], P(('mp', 'dp'))
- gains_weight: float32 [2, 2048], replicated
- scoring_weight: float32 [2, 2048, 2048], P(None, 'dp', 'mp')
- mixing_weight: float32 [2, 2048, 4096], P(None, 'dp', 'mp')
- output_weight: float32 [4096, 2048], P(('mp', 'dp'))
- expand_weight: float32 [2048, 4096], P('dp', 'mp')
- shrink_weight: float32 [4096, 2048], P(('mp', 'dp'))
- scoring_copy: bfloat16 [2, 2048, 2048], P(None, 'dp', 'mp')
- mixing_copy: bfloat16 [2, 2048, 4096], P(None, 'dp', 'mp')
- output_copy: bfloat16 [4096, 2048], P(('mp', 'dp'))
- expand_copy: bfloat16 [2048, 4096], P('dp', 'mp')
- shrink_copy: bfloat16 [4096, 2048], P(('mp', 'dp'))
- trust_norms: float32 [2, 9], replicated
The draws below stay inside these ranges and needn't reach their ends.
Inputs may be any that keep to these rules, and one draw needn't show every extreme that they name: `cotangent`: entries of either sign. `scoring_master`: entries of either sign. `mixing_master`: entries of either sign. `output_master`: entries of either sign. `expand_master`: entries of either sign. `shrink_master`: entries of either sign. `scoring_second`: positive entries. `mixing_second`: positive entries. `output_second`: positive entries. `expand_second`: positive entries. `shrink_second`: positive entries.
All inputs are finite; a program needn't handle non-finite values.
Results may differ from the reference program's by a relative error of at most 0.017.
The reference program's roundings to bfloat16 on the way count: a program that leaves them out, or rounds other values in their place, can miss the bound.
Values may be sent and summed in bfloat16 or wider, within the bound.
A program may use at most 256 MiB of HBM per device.

```python
import math
import jax
import jax.numpy as jnp
from jax import lax

D = 2048
H = 8
DK = 256
DV = 512
FF = 4096
LEN = 1024
TOKENS = 8192
N_DP = 8


def field(key, rows_count, cols_count, spread):
    row_key, col_key = jax.random.split(key)
    row_scale = jnp.exp(jax.random.uniform(row_key, (rows_count, 1), jnp.float32, -spread, spread))
    row_scale = row_scale * 3.0 ** (jnp.arange(rows_count, dtype=jnp.float32)[:, None] / rows_count - 0.5)
    col_scale = jnp.exp(jax.random.uniform(col_key, (1, cols_count), jnp.float32, -spread, spread))
    col_scale = col_scale * 3.0 ** (jnp.arange(cols_count, dtype=jnp.float32)[None, :] / cols_count - 0.5)
    return row_scale * col_scale


def master(key, shape, rows_count, cols_count, fan_in):
    core_key, field_key = jax.random.split(key)
    core = jnp.clip(jax.random.normal(core_key, shape, jnp.float32), -4.0, 4.0)
    spread = 0.5
    return core * field(field_key, rows_count, cols_count, spread) * fan_in ** (-0.5)


def second_moment(key, shape, rows_count, cols_count, level):
    noise_key, field_key = jax.random.split(key)
    noise = jnp.exp(jax.random.uniform(noise_key, shape, jnp.float32, -0.7, 0.7))
    return level * noise * field(field_key, rows_count, cols_count, 0.5)


def draw_cotangent(key, part):
    base_key, scale_key = jax.random.split(jax.random.fold_in(key, 3))
    base = jnp.clip(jax.random.normal(base_key, (TOKENS, D), jnp.float32), -5.0, 5.0)
    scale = jnp.exp(jax.random.uniform(scale_key, (TOKENS, 1), jnp.float32, -0.5, 0.5))
    ramp = 3.0 ** (jnp.arange(TOKENS, dtype=jnp.float32)[:, None] / TOKENS - 0.5)
    return (base * scale * ramp).astype(jnp.bfloat16)


def draw_scoring_master(key, part):
    return master(jax.random.fold_in(key, 11), (2, D, H * DK), D, H * DK, D)


def draw_mixing_master(key, part):
    return master(jax.random.fold_in(key, 12), (2, D, H * DV), D, H * DV, D)


def draw_output_master(key, part):
    return master(jax.random.fold_in(key, 13), (H * DV, D), H * DV, D, H * DV)


def draw_expand_master(key, part):
    return master(jax.random.fold_in(key, 14), (D, FF), D, FF, D)


def draw_shrink_master(key, part):
    return master(jax.random.fold_in(key, 15), (FF, D), FF, D, FF)


def draw_scoring_second(key, part):
    return second_moment(jax.random.fold_in(key, 21), (2, D, H * DK), D, H * DK, 0.001 * TOKENS)


def draw_mixing_second(key, part):
    return second_moment(jax.random.fold_in(key, 22), (2, D, H * DV), D, H * DV, 0.0002 * TOKENS)


def draw_output_second(key, part):
    return second_moment(jax.random.fold_in(key, 23), (H * DV, D), H * DV, D, 0.00049 * TOKENS)


def draw_expand_second(key, part):
    return second_moment(jax.random.fold_in(key, 24), (D, FF), D, FF, 0.00012 * TOKENS)


def draw_shrink_second(key, part):
    return second_moment(jax.random.fold_in(key, 25), (FF, D), FF, D, 0.00036 * TOKENS)


def block_levels(stream_key, shape, cuts, low, top_value):
    factor_of, own = 1.0, jax.random.fold_in(stream_key, 6)
    for dim, blocks in cuts:
        steps = jnp.exp(jax.random.uniform(jax.random.fold_in(own, dim), (blocks,), jnp.float32, low / len(cuts), top_value / len(cuts)))
        factor_of = factor_of * jnp.repeat(steps, shape[dim] // blocks).reshape([-1 if axis == dim else 1 for axis in range(len(shape))])
    return factor_of


def normal_values(stream_key, extent, deviation, most, shards=(), kind=jnp.bfloat16):
    loudness = block_levels(stream_key, extent, shards, -0.22, 0.18) if shards else 1.0
    drawn = jax.random.normal(stream_key, extent, jnp.float32) * deviation * loudness
    return jnp.minimum(jnp.maximum(drawn, -most), most).astype(kind)


def setup_inputs(seed: int = 0) -> dict:
    seeds = jax.random.split(jax.random.key(seed), 21)
    return {
        "tokens": normal_values(seeds[0], (TOKENS, D), 1.0, 6.0, ((0, 32),)),
        "cotangent": draw_cotangent(jax.random.fold_in(seeds[20], 71), 0),
        "gains_master": jnp.clip(1.0 + 0.1 * jax.random.normal(seeds[2], (2, D), jnp.float32), 0.5, 1.5),
        "scoring_master": draw_scoring_master(jax.random.fold_in(seeds[20], 71), 0),
        "mixing_master": draw_mixing_master(jax.random.fold_in(seeds[20], 71), 0),
        "output_master": draw_output_master(jax.random.fold_in(seeds[20], 71), 0),
        "expand_master": draw_expand_master(jax.random.fold_in(seeds[20], 71), 0),
        "shrink_master": draw_shrink_master(jax.random.fold_in(seeds[20], 71), 0),
        "gains_first": normal_values(seeds[8], (2, D), (0.111 * TOKENS ** 0.5), 64.0, (), jnp.float32),
        "gains_second": jnp.clip(jnp.exp(jax.random.uniform(seeds[9], (2, D), jnp.float32, math.log(4.096), math.log(32.768))), 4.096, 32.768),
        "scoring_first": normal_values(seeds[10], (2, D, H * DK), (0.111 * TOKENS ** 0.5), 64.0, ((1, 8), (2, 4)), jnp.float32),
        "scoring_second": draw_scoring_second(jax.random.fold_in(seeds[20], 71), 0),
        "mixing_first": normal_values(seeds[12], (2, D, H * DV), (0.05 * TOKENS ** 0.5), 28.0, ((1, 8), (2, 4)), jnp.float32),
        "mixing_second": draw_mixing_second(jax.random.fold_in(seeds[20], 71), 0),
        "output_first": normal_values(seeds[14], (H * DV, D), (0.078 * TOKENS ** 0.5), 40.0, ((0, 32),), jnp.float32),
        "output_second": draw_output_second(jax.random.fold_in(seeds[20], 71), 0),
        "expand_first": normal_values(seeds[16], (D, FF), (0.039 * TOKENS ** 0.5), 20.0, ((0, 8), (1, 4)), jnp.float32),
        "expand_second": draw_expand_second(jax.random.fold_in(seeds[20], 71), 0),
        "shrink_first": normal_values(seeds[18], (FF, D), (0.067 * TOKENS ** 0.5), 32.0, ((0, 32),), jnp.float32),
        "shrink_second": draw_shrink_second(jax.random.fold_in(seeds[20], 71), 0),
    }


highest = lax.Precision.HIGHEST
beta_one = 0.9
beta_two = 0.999
lamb_epsilon = 1e-06
decay_rate = 0.01
learn_rate = 0.5
norm_epsilon = 1e-06

@jax.custom_vjp
def low(v):
    return lax.optimization_barrier(v.astype(jnp.bfloat16)).astype(jnp.float32)

@jax.custom_vjp
def low_back(v):
    return v

def low_keep(v):
    return (low(v), None)

def low_pass(kept, grad):
    return (grad,)

def back_keep(v):
    return (v, None)

def back_low(kept, grad):
    return (low(grad),)
low.defvjp(low_keep, low_pass)
low_back.defvjp(back_keep, back_low)

def matmul(left, right):
    return jnp.dot(left, right, precision=highest, preferred_element_type=jnp.float32)

def rms_scale(values, gain_row):
    return values * lax.rsqrt(lax.optimization_barrier(jnp.mean(values * values, axis=-1, keepdims=True)) + norm_epsilon) * gain_row

def rotate(values, direction):
    length, heads, features = values.shape
    half = features // 2
    freqs = 10000.0 ** (-jnp.linspace(0.0, 1.0, half, dtype=jnp.float32))
    angle = jnp.arange(length, dtype=jnp.float32)[:, None] * freqs[None, :]
    cosine = jnp.cos(angle)[:, None, :]
    sine = direction * jnp.sin(angle)[:, None, :]
    pairs = values.reshape(length, heads, half, 2)
    even = pairs[..., 0]
    oddly = pairs[..., 1]
    turned = jnp.stack((even * cosine - oddly * sine, oddly * cosine + even * sine), axis=-1)
    return turned.reshape(length, heads, features)

def decay_table(offset, rows_count, length, decay_logs):
    row_pos = offset + jnp.arange(rows_count, dtype=jnp.int32)
    col_pos = jnp.arange(length, dtype=jnp.int32)
    spacing = (row_pos[:, None] - col_pos[None, :]).astype(jnp.float32)
    return jnp.where(spacing >= 0.0, jnp.exp(decay_logs[:, None, None] * jnp.maximum(spacing, 0.0)), 0.0)

def gate_norm(retained, gate_pre):
    normal = retained * lax.rsqrt(lax.optimization_barrier(jnp.mean(retained * retained, axis=-1, keepdims=True)) + norm_epsilon)
    return jax.nn.silu(gate_pre) * normal

def layer(sequence, gains, scoring, mixing, output, expand, shrink):
    length = sequence.shape[0]
    normed = low(rms_scale(sequence, gains[0]))
    queries = low_back(matmul(normed, scoring[0]))
    keys_pre = low_back(matmul(normed, scoring[1]))
    values = low(low_back(matmul(normed, mixing[0]))).reshape(length, H, DV)
    gate_pre = low_back(matmul(normed, mixing[1])).reshape(length, H, DV)
    turned_queries = low(rotate(queries.reshape(length, H, DK), 1.0))
    turned_keys = low(rotate(keys_pre.reshape(length, H, DK), 1.0))
    decay_logs = jnp.log(1.0 - 2.0 ** (-5.0 - jnp.arange(H, dtype=jnp.float32)))
    scores = jnp.einsum('qhd,khd->hqk', turned_queries, turned_keys, precision=highest)
    weights = low(low_back(scores) * decay_table(0, length, length, decay_logs))
    retained = low_back(jnp.einsum('hqk,khe->qhe', weights, values, precision=highest))
    mixed_rows = low(gate_norm(retained, gate_pre).reshape(length, H * DV))
    hidden = sequence + low_back(matmul(mixed_rows, output))
    second_in = low(rms_scale(hidden, gains[1]))
    upward = low_back(matmul(second_in, expand))
    active = low(jax.nn.gelu(upward, approximate=False))
    return hidden + low_back(matmul(active, shrink))

def as_low(weight):
    return weight.astype(jnp.bfloat16).astype(jnp.float32)

def lamb_parts(weight, grad, first, second):
    moment = beta_one * first + (1.0 - beta_one) * grad
    square = beta_two * second + (1.0 - beta_two) * grad * grad
    update = moment / (jnp.sqrt(square) + lamb_epsilon) + decay_rate * weight
    return (moment, square, update)

def reference(tokens, cotangent, gains_master, scoring_master, mixing_master, output_master, expand_master, shrink_master, gains_first, gains_second, scoring_first, scoring_second, mixing_first, mixing_second, output_first, output_second, expand_first, expand_second, shrink_first, shrink_second):
    params = (gains_master, as_low(scoring_master), as_low(mixing_master), as_low(output_master), as_low(expand_master), as_low(shrink_master))
    inputs = tokens.astype(jnp.float32).reshape(N_DP, LEN, D)
    backs = cotangent.astype(jnp.float32).reshape(N_DP, LEN, D)

    def one_sequence(totals, inputs_pair):
        result, pull = jax.vjp(layer, inputs_pair[0], *params)
        grads = pull(inputs_pair[1])
        return (jax.tree.map(jnp.add, totals, tuple(grads[1:])), (result.astype(jnp.bfloat16), grads[0]))
    zeros = jax.tree.map(jnp.zeros_like, params)
    totals, (outputs, input_backs) = lax.scan(one_sequence, zeros, (inputs, backs))
    gains_grad, scoring_grad, mixing_grad, output_grad, expand_grad, shrink_grad = totals
    masters = (gains_master, scoring_master, mixing_master, output_master, expand_master, shrink_master)
    grads = (gains_grad, scoring_grad, mixing_grad, output_grad, expand_grad, shrink_grad)
    firsts = (gains_first, scoring_first, mixing_first, output_first, expand_first, shrink_first)
    seconds = (gains_second, scoring_second, mixing_second, output_second, expand_second, shrink_second)
    parts = [lamb_parts(masters[i], grads[i], firsts[i], seconds[i]) for i in range(6)]

    def sums_of(values, stacked):
        if stacked == 1:
            return lax.optimization_barrier(jnp.sum(values * values, axis=1))
        if stacked == 2:
            return lax.optimization_barrier(jnp.sum(values * values, axis=(1, 2)))
        return jnp.sum(values * values)[None]
    kinds = (1, 2, 2, 0, 0, 0)
    weight_sq = [sums_of(masters[i], kinds[i]) for i in range(6)]
    update_sq = [sums_of(parts[i][2], kinds[i]) for i in range(6)]
    order = (1, 2, 3, 4, 5, 0)
    weight_norms = jnp.sqrt(jnp.concatenate([weight_sq[i] for i in order]))
    update_norms = jnp.sqrt(jnp.concatenate([update_sq[i] for i in order]))
    trust_norms = jnp.stack((weight_norms, update_norms))
    ratios = [jnp.sqrt(weight_sq[i]) / jnp.sqrt(update_sq[i]) for i in range(6)]
    shaped = (ratios[0][:, None], ratios[1][:, None, None], ratios[2][:, None, None], ratios[3][0], ratios[4][0], ratios[5][0])
    news = [masters[i] - learn_rate * shaped[i] * parts[i][2] for i in range(6)]
    layer_output = outputs.reshape(N_DP * LEN, D)
    input_grad = input_backs.reshape(N_DP * LEN, D)
    return (layer_output, input_grad, gains_grad, scoring_grad, mixing_grad, output_grad, expand_grad, shrink_grad, parts[0][0], parts[1][0], parts[2][0], parts[3][0], parts[4][0], parts[5][0], parts[0][1], parts[1][1], parts[2][1], parts[3][1], parts[4][1], parts[5][1], news[0], news[1], news[2], news[3], news[4], news[5], news[1].astype(jnp.bfloat16), news[2].astype(jnp.bfloat16), news[3].astype(jnp.bfloat16), news[4].astype(jnp.bfloat16), news[5].astype(jnp.bfloat16), trust_norms)
```

```python
import jax
import jax.numpy as jnp
from jax import lax
from jax.sharding import PartitionSpec as P

DK = 256
DV = 512


beta_one = 0.9
beta_two = 0.999
lamb_epsilon = 1e-06
decay_rate = 0.01
learn_rate = 0.5
norm_epsilon = 1e-06


def rms_scale(values, gain_row):
    return (
        values
        * lax.rsqrt(jnp.mean(values * values, axis=-1, keepdims=True) + norm_epsilon)
        * gain_row
    )


def turn(values, cosine, sine):
    half = values.shape[1] // 2
    even = values[:, :half]
    oddly = values[:, half:]
    return jnp.concatenate((even * cosine - oddly * sine, oddly * cosine + even * sine), axis=1)


def split_order(features):
    old = lax.broadcasted_iota(jnp.int32, (features, features), 0)
    new = lax.broadcasted_iota(jnp.int32, (features, features), 1)
    head, place = new // DK, new % DK
    half = DK // 2
    source = head * DK + jnp.where(place < half, 2 * place, 2 * (place - half) + 1)
    return (old == source).astype(jnp.bfloat16)


def gate_norm(retained, gate_pre):
    normal = retained * lax.rsqrt(
        jnp.mean(retained * retained, axis=-1, keepdims=True) + norm_epsilon
    )
    return jax.nn.silu(gate_pre) * normal


def gelu_exact(values):
    return jax.nn.gelu(values, approximate=False)


def plain_dot(left, right):
    return jnp.dot(left, right, preferred_element_type=jnp.float32)


def contract_rows(left, right):
    return lax.dot_general(
        left, right, (((0,), (0,)), ((), ())), preferred_element_type=jnp.float32
    )


def contract_cols(left, right):
    return lax.dot_general(
        left, right, (((1,), (1,)), ((), ())), preferred_element_type=jnp.float32
    )


def swap(values, axis, bit):
    return lax.ppermute(values, axis, [(i, i ^ bit) for i in range(lax.axis_size(axis))])


def gather_rows(block):
    far = swap(block, "mp", 2)
    near = swap(block, "mp", 1)
    last = swap(far, "mp", 1)
    return jnp.concatenate((block, near, far, last), axis=0)


def scatter_rows(parts):
    rows = parts.shape[0] // 4
    block = [parts[k * rows : (k + 1) * rows] for k in range(4)]
    across = block[2] + swap(block[3], "mp", 1)
    far = swap(across.astype(jnp.bfloat16), "mp", 2)
    return block[0] + swap(block[1], "mp", 1) + far.astype(jnp.float32)


def sum_everywhere(values):
    for axis in ("mp", "dp"):
        bit = 1
        while bit < lax.axis_size(axis):
            values = values + swap(values, axis, bit)
            bit *= 2
    return values


def gather_weights(shard):
    return lax.all_gather(shard, "dp", axis=0, tiled=True)


def scatter_grads(local):
    return lax.psum_scatter(
        local.astype(jnp.bfloat16), "dp", scatter_dimension=0, tiled=True
    )


def lamb_parts(weight, grad, first, second):
    moment = beta_one * first + (1.0 - beta_one) * grad
    square = beta_two * second + (1.0 - beta_two) * grad * grad
    update = moment / (jnp.sqrt(square) + lamb_epsilon) + decay_rate * weight
    return (moment, square, update)


def body(
    tokens,
    cotangent,
    gains_master,
    scoring_master,
    mixing_master,
    output_master,
    expand_master,
    shrink_master,
    gains_first,
    gains_second,
    scoring_first,
    scoring_second,
    mixing_first,
    mixing_second,
    output_first,
    output_second,
    expand_first,
    expand_second,
    shrink_first,
    shrink_second,
):
    low = jnp.bfloat16
    model_devices = lax.axis_size("mp")
    assert model_devices == 4
    rows = tokens.shape[0]
    length = rows * model_devices
    wide = scoring_master.shape[2]
    broad = mixing_master.shape[2]
    heads_local = wide // DK
    mine = lax.axis_index("mp")

    order = split_order(wide)
    qk_shard = jnp.concatenate(
        (
            plain_dot(scoring_master[0].astype(low), order).astype(low),
            plain_dot(scoring_master[1].astype(low), order).astype(low),
        ),
        axis=1,
    )
    qk_low = gather_weights(qk_shard)
    vg_low = gather_weights(
        jnp.concatenate((mixing_master[0].astype(low), mixing_master[1].astype(low)), axis=1)
    )
    output_low = gather_weights(output_master.astype(low))
    expand_low = gather_weights(expand_master.astype(low))
    shrink_low = gather_weights(shrink_master.astype(low))

    place = jnp.concatenate(
        [(mine ^ k) * rows + jnp.arange(rows, dtype=jnp.int32) for k in range(model_devices)]
    )
    half = DK // 2
    freqs = 10000.0 ** (-jnp.linspace(0.0, 1.0, half, dtype=jnp.float32))
    angle = place.astype(jnp.float32)[:, None] * freqs[None, :]
    cosine = jnp.cos(angle)
    sine = jnp.sin(angle)
    spacing = (place[:, None] - place[None, :]).astype(jnp.float32)
    head_ids = mine * heads_local + jnp.arange(heads_local, dtype=jnp.int32)
    decay_logs = jnp.log(1.0 - 2.0 ** (-5.0 - head_ids.astype(jnp.float32)))

    def table(head):
        return jnp.where(
            spacing >= 0.0, jnp.exp(decay_logs[head] * jnp.maximum(spacing, 0.0)), 0.0
        )

    def cols(values, head, width):
        return values[:, head * width : (head + 1) * width]

    inputs = tokens.astype(jnp.float32)
    gain_one = gains_master[0]
    gain_two = gains_master[1]
    normed = rms_scale(inputs, gain_one).astype(low)
    normed_all = gather_rows(normed)
    back_all = gather_rows(cotangent)
    qk = plain_dot(normed_all, qk_low)
    vg = plain_dot(normed_all, vg_low)
    values = vg[:, :broad].astype(low)
    gate_pre = vg[:, broad:]
    turned_q, turned_k, weights, retained, mixed_parts = [], [], [], [], []
    for head in range(heads_local):
        turned_q.append(turn(cols(qk[:, :wide], head, DK), cosine, sine).astype(low))
        turned_k.append(turn(cols(qk[:, wide:], head, DK), cosine, sine).astype(low))
        weights.append((contract_cols(turned_q[-1], turned_k[-1]) * table(head)).astype(low))
        retained.append(plain_dot(weights[-1], cols(values, head, DV)))
        mixed_parts.append(gate_norm(retained[-1], cols(gate_pre, head, DV)).astype(low))
    mixed = jnp.concatenate(mixed_parts, axis=1)
    hidden = inputs + scatter_rows(plain_dot(mixed, output_low))
    second_in = rms_scale(hidden, gain_two).astype(low)
    second_all = gather_rows(second_in)
    upward = plain_dot(second_all, expand_low)
    active = gelu_exact(upward).astype(low)
    shrink_sum = scatter_grads(contract_rows(active, back_all))
    layer_output = (hidden + scatter_rows(plain_dot(active, shrink_low))).astype(low)

    active_back = contract_cols(back_all, shrink_low)
    upward_back = jax.vjp(gelu_exact, upward)[1](active_back)[0].astype(low)
    second_back = scatter_rows(contract_cols(upward_back, expand_low))
    expand_sum = scatter_grads(contract_rows(second_all, upward_back))
    hidden_part, gain_two_grad = jax.vjp(rms_scale, hidden, gain_two)[1](second_back)
    hidden_back = cotangent.astype(jnp.float32) + hidden_part
    branch_all = gather_rows(hidden_back.astype(low))
    mixed_back = contract_cols(branch_all, output_low)
    output_sum = scatter_grads(contract_rows(mixed, branch_all))
    query_parts, keys_parts, values_parts, gate_parts = [], [], [], []
    for head in range(heads_local):
        retained_back, gate_back = jax.vjp(gate_norm, retained[head], cols(gate_pre, head, DV))[1](
            cols(mixed_back, head, DV)
        )
        retained_low = retained_back.astype(low)
        gate_parts.append(gate_back.astype(low))
        score_back = (
            contract_cols(retained_low, cols(values, head, DV)) * table(head)
        ).astype(low)
        query_parts.append(turn(plain_dot(score_back, turned_k[head]), cosine, -sine).astype(low))
        keys_parts.append(turn(contract_rows(score_back, turned_q[head]), cosine, -sine).astype(low))
        values_parts.append(contract_rows(weights[head], retained_low).astype(low))
    gate_back_low = jnp.concatenate(gate_parts, axis=1)
    values_back_low = jnp.concatenate(values_parts, axis=1)
    qk_back_low = jnp.concatenate(query_parts + keys_parts, axis=1)
    gate_sum = scatter_grads(contract_rows(normed_all, gate_back_low))
    values_sum = scatter_grads(contract_rows(normed_all, values_back_low))
    qk_sum = scatter_grads(contract_rows(normed_all, qk_back_low))
    vg_back_low = jnp.concatenate((values_back_low, gate_back_low), axis=1)
    normed_back = scatter_rows(
        contract_cols(qk_back_low, qk_low) + contract_cols(vg_back_low, vg_low)
    )
    inputs_part, gain_one_grad = jax.vjp(rms_scale, inputs, gain_one)[1](normed_back)
    input_grad = hidden_back + inputs_part
    gains_grad = sum_everywhere(jnp.stack((gain_one_grad, gain_two_grad)))

    scoring_grad = jnp.stack(
        (contract_cols(qk_sum[:, :wide], order), contract_cols(qk_sum[:, wide:], order))
    )
    mixing_grad = jnp.stack((values_sum, gate_sum)).astype(jnp.float32)
    output_grad = output_sum.astype(jnp.float32)
    expand_grad = expand_sum.astype(jnp.float32)
    shrink_grad = shrink_sum.astype(jnp.float32)
    scoring_moment, scoring_square, scoring_update = lamb_parts(
        scoring_master, scoring_grad, scoring_first, scoring_second
    )
    mixing_moment, mixing_square, mixing_update = lamb_parts(
        mixing_master, mixing_grad, mixing_first, mixing_second
    )
    output_moment, output_square, output_update = lamb_parts(
        output_master, output_grad, output_first, output_second
    )
    expand_moment, expand_square, expand_update = lamb_parts(
        expand_master, expand_grad, expand_first, expand_second
    )
    shrink_moment, shrink_square, shrink_update = lamb_parts(
        shrink_master, shrink_grad, shrink_first, shrink_second
    )
    gains_moment, gains_square, gains_update = lamb_parts(
        gains_master, gains_grad, gains_first, gains_second
    )
    weight_local = jnp.concatenate(
        (
            jnp.sum(scoring_master * scoring_master, axis=(1, 2)),
            jnp.sum(mixing_master * mixing_master, axis=(1, 2)),
            jnp.stack(
                (
                    jnp.sum(output_master * output_master),
                    jnp.sum(expand_master * expand_master),
                    jnp.sum(shrink_master * shrink_master),
                )
            ),
        )
    )
    update_local = jnp.concatenate(
        (
            jnp.sum(scoring_update * scoring_update, axis=(1, 2)),
            jnp.sum(mixing_update * mixing_update, axis=(1, 2)),
            jnp.stack(
                (
                    jnp.sum(output_update * output_update),
                    jnp.sum(expand_update * expand_update),
                    jnp.sum(shrink_update * shrink_update),
                )
            ),
        )
    )
    weight_total, update_total = sum_everywhere(jnp.stack((weight_local, update_local)))
    weight_norms = jnp.sqrt(weight_total)
    update_norms = jnp.sqrt(update_total)
    ratios = weight_norms / update_norms
    gains_wnorm = jnp.sqrt(jnp.sum(gains_master * gains_master, axis=1))
    gains_unorm = jnp.sqrt(jnp.sum(gains_update * gains_update, axis=1))
    scoring_weight = scoring_master - learn_rate * ratios[0:2][:, None, None] * scoring_update
    mixing_weight = mixing_master - learn_rate * ratios[2:4][:, None, None] * mixing_update
    output_weight = output_master - learn_rate * ratios[4] * output_update
    expand_weight = expand_master - learn_rate * ratios[5] * expand_update
    shrink_weight = shrink_master - learn_rate * ratios[6] * shrink_update
    gains_weight = gains_master - learn_rate * (gains_wnorm / gains_unorm)[:, None] * gains_update
    trust_norms = jnp.stack(
        (jnp.concatenate((weight_norms, gains_wnorm)), jnp.concatenate((update_norms, gains_unorm)))
    )
    return (
        layer_output,
        input_grad,
        gains_grad,
        scoring_grad,
        mixing_grad,
        output_grad,
        expand_grad,
        shrink_grad,
        gains_moment,
        scoring_moment,
        mixing_moment,
        output_moment,
        expand_moment,
        shrink_moment,
        gains_square,
        scoring_square,
        mixing_square,
        output_square,
        expand_square,
        shrink_square,
        gains_weight,
        scoring_weight,
        mixing_weight,
        output_weight,
        expand_weight,
        shrink_weight,
        scoring_weight.astype(jnp.bfloat16),
        mixing_weight.astype(jnp.bfloat16),
        output_weight.astype(jnp.bfloat16),
        expand_weight.astype(jnp.bfloat16),
        shrink_weight.astype(jnp.bfloat16),
        trust_norms,
    )


def solution(mesh):
    placed = (
        P(("dp", "mp"), None),
        P(("dp", "mp"), None),
        P(),
        P(None, "dp", "mp"),
        P(None, "dp", "mp"),
        P(("mp", "dp"), None),
        P("dp", "mp"),
        P(("mp", "dp"), None),
        P(),
        P(),
        P(None, "dp", "mp"),
        P(None, "dp", "mp"),
        P(None, "dp", "mp"),
        P(None, "dp", "mp"),
        P(("mp", "dp"), None),
        P(("mp", "dp"), None),
        P("dp", "mp"),
        P("dp", "mp"),
        P(("mp", "dp"), None),
        P(("mp", "dp"), None),
    )
    return jax.shard_map(
        body,
        mesh=mesh,
        in_specs=placed,
        out_specs=(
            P(("dp", "mp"), None),
            P(("dp", "mp"), None),
            P(),
            P(None, "dp", "mp"),
            P(None, "dp", "mp"),
            P(("mp", "dp"), None),
            P("dp", "mp"),
            P(("mp", "dp"), None),
            P(),
            P(None, "dp", "mp"),
            P(None, "dp", "mp"),
            P(("mp", "dp"), None),
            P("dp", "mp"),
            P(("mp", "dp"), None),
            P(),
            P(None, "dp", "mp"),
            P(None, "dp", "mp"),
            P(("mp", "dp"), None),
            P("dp", "mp"),
            P(("mp", "dp"), None),
            P(),
            P(None, "dp", "mp"),
            P(None, "dp", "mp"),
            P(("mp", "dp"), None),
            P("dp", "mp"),
            P(("mp", "dp"), None),
            P(None, "dp", "mp"),
            P(None, "dp", "mp"),
            P(("mp", "dp"), None),
            P("dp", "mp"),
            P(("mp", "dp"), None),
            P(),
        ),
        check_vma=False,
    )
```

```python
import jax
import jax.numpy as jnp
from jax import lax
from jax.experimental.layout import Layout, with_layout_constraint
from jax.sharding import PartitionSpec as P


DK = 256
DV = 512


beta_one = 0.9
beta_two = 0.999
lamb_epsilon = 1e-06
decay_rate = 0.01
learn_rate = 0.5
norm_epsilon = 1e-06


def rms_scale(values, gain_row):
    return (
        values
        * lax.rsqrt(jnp.mean(values * values, axis=-1, keepdims=True) + norm_epsilon)
        * gain_row
    )


def turn(values, cosine, sine):
    half = values.shape[1] // 2
    even = values[:, :half]
    oddly = values[:, half:]
    return jnp.concatenate((even * cosine - oddly * sine, oddly * cosine + even * sine), axis=1)


def split_order(features):
    old = lax.broadcasted_iota(jnp.int32, (features, features), 0)
    new = lax.broadcasted_iota(jnp.int32, (features, features), 1)
    head, place = new // DK, new % DK
    half = DK // 2
    source = head * DK + jnp.where(place < half, 2 * place, 2 * (place - half) + 1)
    return (old == source).astype(jnp.bfloat16)


def gate_norm(retained, gate_pre):
    normal = retained * lax.rsqrt(
        jnp.mean(retained * retained, axis=-1, keepdims=True) + norm_epsilon
    )
    return jax.nn.silu(gate_pre) * normal


def gelu_exact(values):
    return jax.nn.gelu(values, approximate=False)


def plain_dot(left, right):
    return jnp.dot(left, right, preferred_element_type=jnp.float32)


def contract_rows(left, right):
    return lax.dot_general(
        left, right, (((0,), (0,)), ((), ())), preferred_element_type=jnp.float32
    )


def contract_cols(left, right):
    return lax.dot_general(
        left, right, (((1,), (1,)), ((), ())), preferred_element_type=jnp.float32
    )


def swap(values, axis, bit):
    return lax.ppermute(values, axis, [(i, i ^ bit) for i in range(lax.axis_size(axis))])


def gather_rows(block):
    far = swap(block, "mp", 2)
    near = swap(block, "mp", 1)
    last = swap(far, "mp", 1)
    return jnp.concatenate((block, near, far, last), axis=0)


def scatter_rows(parts):
    rows = parts.shape[0] // 4
    block = [parts[k * rows : (k + 1) * rows] for k in range(4)]
    across = block[2] + swap(block[3], "mp", 1)
    far = swap(across.astype(jnp.bfloat16), "mp", 2)
    near = swap(block[1], "mp", 1)
    return block[0] + near + far.astype(jnp.float32)


def sum_everywhere(values):
    for axis in ("mp", "dp"):
        bit = 1
        while bit < lax.axis_size(axis):
            values = values + swap(values, axis, bit)
            bit *= 2
    return values


def outer_groups():
    count = lax.axis_size("dp")
    return [list(range(0, count, 2)), list(range(1, count, 2))]


def after(values, *others):
    return lax.optimization_barrier((values, *others))[0]


def gather_outer(shard):
    return lax.all_gather(
        shard, "dp", axis=0, tiled=False, axis_index_groups=outer_groups()
    )


def gather_inner(mine):
    other = swap(mine, "dp", 1)
    first = after(lax.axis_index("dp") % 2 == 0, other)
    both = jnp.stack((jnp.where(first, mine, other), jnp.where(first, other, mine)), axis=1)
    return both.reshape(-1, mine.shape[2])


def scatter_whole(left, right):
    local = contract_rows(left, right).astype(jnp.bfloat16)
    return local, lax.psum_scatter(local, "dp", scatter_dimension=0, tiled=True)


def scatter_inner(left, right):
    local = contract_rows(left, right).astype(jnp.bfloat16)
    count = lax.axis_size("dp")
    parts = local.reshape(count // 2, 2, -1, local.shape[1])
    first = after(lax.axis_index("dp") % 2 == 0, local)
    kept = jnp.where(first, parts[:, 0], parts[:, 1])
    given = jnp.where(first, parts[:, 1], parts[:, 0])
    taken = swap(given, "dp", 1)
    return (kept + taken).reshape(-1, local.shape[1]), given


def scatter_outer(halves):
    return lax.psum_scatter(
        halves, "dp", scatter_dimension=0, tiled=True, axis_index_groups=outer_groups()
    )


def lamb_parts(weight, grad, first, second):
    moment = beta_one * first + (1.0 - beta_one) * grad
    square = beta_two * second + (1.0 - beta_two) * grad * grad
    update = moment / (jnp.sqrt(square) + lamb_epsilon) + decay_rate * weight
    return (moment, square, update)


def body(
    tokens,
    cotangent,
    gains_master,
    scoring_master,
    mixing_master,
    output_master,
    expand_master,
    shrink_master,
    gains_first,
    gains_second,
    scoring_first,
    scoring_second,
    mixing_first,
    mixing_second,
    output_first,
    output_second,
    expand_first,
    expand_second,
    shrink_first,
    shrink_second,
):
    low = jnp.bfloat16
    model_devices = lax.axis_size("mp")
    assert model_devices == 4
    rows = tokens.shape[0]
    wide = scoring_master.shape[2]
    heads_local = wide // DK
    mine = lax.axis_index("mp")

    order = split_order(wide)
    qk_shard = jnp.concatenate(
        (
            plain_dot(scoring_master[0].astype(low), order).astype(low),
            plain_dot(scoring_master[1].astype(low), order).astype(low),
        ),
        axis=1,
    )
    qk_shard = with_layout_constraint(qk_shard, Layout(major_to_minor=(0, 1)))
    qk_outer = gather_outer(qk_shard)
    v_outer = gather_outer(mixing_master[0].astype(low))
    g_outer = gather_outer(mixing_master[1].astype(low))
    output_outer = gather_outer(output_master.astype(low))
    expand_outer = gather_outer(expand_master.astype(low))
    shrink_outer = gather_outer(shrink_master.astype(low))
    qk_low = gather_inner(qk_outer)
    v_low = gather_inner(v_outer)
    g_low = gather_inner(g_outer)
    output_low = gather_inner(output_outer)
    expand_low = gather_inner(expand_outer)
    shrink_low = gather_inner(shrink_outer)

    place = jnp.concatenate(
        [(mine ^ k) * rows + jnp.arange(rows, dtype=jnp.int32) for k in range(model_devices)]
    )
    half = DK // 2
    freqs = 10000.0 ** (-jnp.linspace(0.0, 1.0, half, dtype=jnp.float32))
    angle = place.astype(jnp.float32)[:, None] * freqs[None, :]
    cosine = jnp.cos(angle)
    sine = jnp.sin(angle)
    spacing = (place[:, None] - place[None, :]).astype(jnp.float32)
    head_ids = mine * heads_local + jnp.arange(heads_local, dtype=jnp.int32)
    decay_logs = jnp.log(1.0 - 2.0 ** (-5.0 - head_ids.astype(jnp.float32)))

    def table(head):
        return jnp.where(
            spacing >= 0.0, jnp.exp(decay_logs[head] * jnp.maximum(spacing, 0.0)), 0.0
        )

    def cols(values, head, width):
        return values[:, head * width : (head + 1) * width]

    inputs = tokens.astype(jnp.float32)
    gain_one = gains_master[0]
    gain_two = gains_master[1]
    normed = rms_scale(inputs, gain_one).astype(low)
    normed_all = gather_rows(normed)
    back_all = gather_rows(cotangent)
    qk = plain_dot(normed_all, qk_low)
    values = plain_dot(normed_all, v_low).astype(low)
    gate_pre = plain_dot(normed_all, g_low)
    turned_q, turned_k, weights, retained, mixed_parts = [], [], [], [], []
    for head in range(heads_local):
        turned_q.append(turn(cols(qk[:, :wide], head, DK), cosine, sine).astype(low))
        turned_k.append(turn(cols(qk[:, wide:], head, DK), cosine, sine).astype(low))
        weights.append((contract_cols(turned_q[-1], turned_k[-1]) * table(head)).astype(low))
        retained.append(plain_dot(weights[-1], cols(values, head, DV)))
        mixed_parts.append(gate_norm(retained[-1], cols(gate_pre, head, DV)).astype(low))
    mixed = jnp.concatenate(mixed_parts, axis=1)
    branch = plain_dot(after(mixed, back_all), output_low)
    hidden = inputs + scatter_rows(branch)
    second_in = rms_scale(hidden, gain_two).astype(low)
    second_all = gather_rows(second_in)
    upward = plain_dot(second_all, expand_low)
    active = lax.optimization_barrier(gelu_exact(upward).astype(low))
    shrink_local, shrink_sum = scatter_whole(active, back_all)

    active_back = contract_cols(after(back_all, shrink_local), shrink_low)
    upward_back = jax.vjp(gelu_exact, upward)[1](active_back)[0].astype(low)
    fold = contract_cols(upward_back, expand_low)
    second_back = scatter_rows(fold)
    expand_halves, _ = scatter_inner(second_all, upward_back)
    hidden_part, gain_two_grad = jax.vjp(rms_scale, hidden, gain_two)[1](second_back)
    hidden_back = cotangent.astype(jnp.float32) + hidden_part
    branch_all = gather_rows(hidden_back.astype(low))
    output_halves, output_given = scatter_inner(mixed, branch_all)
    mixed_back = contract_cols(after(branch_all, output_given), output_low)
    result = plain_dot(active, shrink_low)
    layer_output = (after(hidden, branch_all) + scatter_rows(result)).astype(low)
    query_parts, keys_parts, values_parts, gate_parts, retained_lows = [], [], [], [], []
    for head in range(heads_local):
        retained_back, gate_back = jax.vjp(gate_norm, retained[head], cols(gate_pre, head, DV))[1](
            cols(mixed_back, head, DV)
        )
        retained_lows.append(retained_back.astype(low))
        gate_parts.append(gate_back.astype(low))
    gate_back_low = jnp.concatenate(gate_parts, axis=1)
    expand_sum = scatter_outer(expand_halves)
    gate_halves, gate_given = scatter_inner(normed_all, gate_back_low)
    retained_lows[0] = after(retained_lows[0], expand_halves, output_given)
    retained_lows[1] = after(retained_lows[1], gate_given)
    ready = (expand_halves, output_halves)
    for head in range(heads_local):
        retained_low = retained_lows[head]
        score_back = (contract_cols(retained_low, cols(values, head, DV)) * table(head)).astype(low)
        score_back = after(score_back, ready[head])
        query_back = plain_dot(score_back, turned_k[head])
        key_back = contract_rows(score_back, turned_q[head])
        query_parts.append(turn(query_back, cosine, -sine).astype(low))
        keys_parts.append(turn(key_back, cosine, -sine).astype(low))
        values_parts.append(contract_rows(weights[head], retained_low).astype(low))
    values_back_low = jnp.concatenate(values_parts, axis=1)
    qk_back_low = jnp.concatenate(query_parts + keys_parts, axis=1)
    values_halves, values_given = scatter_inner(normed_all, values_back_low)
    qk_halves, qk_given = scatter_inner(normed_all, qk_back_low)
    output_sum = scatter_outer(output_halves)
    total = contract_cols(after(gate_back_low, layer_output, values_given, qk_given), g_low)
    total = total + contract_cols(values_back_low, v_low)
    total = total + contract_cols(qk_back_low, qk_low)
    gate_sum = scatter_outer(gate_halves)
    normed_back = scatter_rows(after(total, gate_halves))
    inputs_part, gain_one_grad = jax.vjp(rms_scale, inputs, gain_one)[1](normed_back)
    input_grad = hidden_back + inputs_part
    values_sum = scatter_outer(values_halves)
    gains_grad = sum_everywhere(jnp.stack((gain_one_grad, gain_two_grad)))
    qk_sum = scatter_outer(qk_halves)

    mixing_grad = jnp.stack((values_sum, gate_sum)).astype(jnp.float32)
    output_grad = output_sum.astype(jnp.float32)
    expand_grad = expand_sum.astype(jnp.float32)
    shrink_grad = shrink_sum.astype(jnp.float32)
    output_master = after(output_master, output_sum)
    expand_master = after(expand_master, expand_sum)
    shrink_master = after(shrink_master, shrink_sum)
    mixing_master = after(mixing_master, gate_sum)
    scoring_master = after(scoring_master, gate_sum)
    mixing_moment, mixing_square, mixing_update = lamb_parts(
        mixing_master, mixing_grad, mixing_first, mixing_second
    )
    output_moment, output_square, output_update = lamb_parts(
        output_master, output_grad, output_first, output_second
    )
    expand_moment, expand_square, expand_update = lamb_parts(
        expand_master, expand_grad, expand_first, expand_second
    )
    shrink_moment, shrink_square, shrink_update = lamb_parts(
        shrink_master, shrink_grad, shrink_first, shrink_second
    )
    gains_moment, gains_square, gains_update = lamb_parts(
        gains_master, gains_grad, gains_first, gains_second
    )

    def square_sums(stacked, *single):
        sums = [jnp.sum(stacked[i] * stacked[i]) for i in range(stacked.shape[0])]
        return sums + [jnp.sum(one * one) for one in single]

    early_parts = jnp.stack(
        square_sums(scoring_master)
        + square_sums(mixing_master, output_master, expand_master, shrink_master)
        + [jnp.sum(one * one) for one in (output_update, expand_update, shrink_update)]
    )
    early_sums = sum_everywhere(early_parts)
    early_norms = jnp.sqrt(early_sums)
    weight_norms = early_norms[:7]
    ratios = weight_norms[4:] / early_norms[7:]
    gains_wnorm = jnp.sqrt(jnp.sum(gains_master * gains_master, axis=1))
    gains_unorm = jnp.sqrt(jnp.sum(gains_update * gains_update, axis=1))
    output_weight = output_master - learn_rate * ratios[0] * output_update
    expand_weight = expand_master - learn_rate * ratios[1] * expand_update
    shrink_weight = shrink_master - learn_rate * ratios[2] * shrink_update
    mixing_sums = jnp.sum(mixing_update * mixing_update, axis=(1, 2))
    gains_weight = gains_master - learn_rate * (gains_wnorm / gains_unorm)[:, None] * gains_update

    qk_last = after(qk_sum, mixing_sums, output_weight, expand_weight, shrink_weight)
    scoring_grad = jnp.stack(
        (contract_cols(qk_last[:, :wide], order), contract_cols(qk_last[:, wide:], order))
    )
    scoring_moment, scoring_square, scoring_update = lamb_parts(
        scoring_master, scoring_grad, scoring_first, scoring_second
    )
    scoring_sums = jnp.sum(scoring_update * scoring_update, axis=(1, 2))
    late_norms = jnp.sqrt(sum_everywhere(jnp.stack((scoring_sums, mixing_sums)))).reshape(4)
    late_ratios = (weight_norms[:4] / late_norms)[:, None, None]
    scoring_weight = scoring_master - learn_rate * late_ratios[:2] * scoring_update
    mixing_weight = mixing_master - learn_rate * late_ratios[2:] * mixing_update
    update_norms = jnp.concatenate((late_norms, early_norms[7:]))
    trust_norms = jnp.stack(
        (jnp.concatenate((weight_norms, gains_wnorm)), jnp.concatenate((update_norms, gains_unorm)))
    )
    return (
        layer_output,
        input_grad,
        gains_grad,
        scoring_grad,
        mixing_grad,
        output_grad,
        expand_grad,
        shrink_grad,
        gains_moment,
        scoring_moment,
        mixing_moment,
        output_moment,
        expand_moment,
        shrink_moment,
        gains_square,
        scoring_square,
        mixing_square,
        output_square,
        expand_square,
        shrink_square,
        gains_weight,
        scoring_weight,
        mixing_weight,
        output_weight,
        expand_weight,
        shrink_weight,
        scoring_weight.astype(jnp.bfloat16),
        mixing_weight.astype(jnp.bfloat16),
        output_weight.astype(jnp.bfloat16),
        expand_weight.astype(jnp.bfloat16),
        shrink_weight.astype(jnp.bfloat16),
        trust_norms,
    )


def solution(mesh):
    placed = (
        P(("dp", "mp"), None),
        P(("dp", "mp"), None),
        P(),
        P(None, "dp", "mp"),
        P(None, "dp", "mp"),
        P(("mp", "dp"), None),
        P("dp", "mp"),
        P(("mp", "dp"), None),
        P(),
        P(),
        P(None, "dp", "mp"),
        P(None, "dp", "mp"),
        P(None, "dp", "mp"),
        P(None, "dp", "mp"),
        P(("mp", "dp"), None),
        P(("mp", "dp"), None),
        P("dp", "mp"),
        P("dp", "mp"),
        P(("mp", "dp"), None),
        P(("mp", "dp"), None),
    )


    return jax.shard_map(
        body,
        mesh=mesh,
        in_specs=placed,
        out_specs=(
            P(("dp", "mp"), None),
            P(("dp", "mp"), None),
            P(),
            P(None, "dp", "mp"),
            P(None, "dp", "mp"),
            P(("mp", "dp"), None),
            P("dp", "mp"),
            P(("mp", "dp"), None),
            P(),
            P(None, "dp", "mp"),
            P(None, "dp", "mp"),
            P(("mp", "dp"), None),
            P("dp", "mp"),
            P(("mp", "dp"), None),
            P(),
            P(None, "dp", "mp"),
            P(None, "dp", "mp"),
            P(("mp", "dp"), None),
            P("dp", "mp"),
            P(("mp", "dp"), None),
            P(),
            P(None, "dp", "mp"),
            P(None, "dp", "mp"),
            P(("mp", "dp"), None),
            P("dp", "mp"),
            P(("mp", "dp"), None),
            P(None, "dp", "mp"),
            P(None, "dp", "mp"),
            P(("mp", "dp"), None),
            P("dp", "mp"),
            P(("mp", "dp"), None),
            P(),
        ),
        check_vma=False,
    )
```
